512 devices in a mesh: loop: 32 (over z, x_hi, core), rep: 16 (over x_lo, y).
Axes of the slice: x: 4 (x_hi: 2, x_lo: 2; x = x_hi * 2 + x_lo), y: 8, z: 8, core: 2. Of those that a mesh axis runs over, the one named last changes fastest.
Arguments:
- lam: bfloat16 [8, 384, 16384], P(None, None, ('rep', 'loop')), may hold values from -6 to 6
- integrals: bfloat16 [8, 16384, 8192], P(None, 'rep', 'loop'), may hold values from -0.046875 to 0.046875
- block_mask: int32 [8, 512], P(None, 'rep'), may hold values 0 or 1
Outputs:
- ladder: bfloat16 [8, 384, 8192], P(None, 'rep', 'loop')
The draws below stay inside these ranges and needn't reach their ends.
All inputs are finite; a program needn't handle non-finite values. No bound on the sum of `block_mask` on one device may be relied on, other than what follows from the above.
Results may differ from the reference program's by a relative error of at most 0.001.
Values may be sent and summed in bfloat16 or wider, within the bound.
A program may use at most 64 MiB of HBM per device.

```python
import jax
import jax.numpy as jnp
from jax import lax

NIRREP = 8
OCC_PAIRS = 384
CBH = 32
CDBLOCKS = 512
CDH = 16384
ABH = 8192


def place_ends(drawn, rng, least, top_value):
    longest = drawn.shape.index(max(drawn.shape))
    spots = []
    for shift in (0, 1):
        where = [jax.random.randint(jax.random.fold_in(rng, axis), (), 0, length) for axis, length in enumerate(drawn.shape)]
        where[longest] = (where[longest] + shift) % drawn.shape[longest]
        spots.append(tuple(where))
    return drawn.at[spots[0]].set(least).at[spots[1]].set(top_value)


def steps_of(key, extent, pieces, low, top_value):
    loudness = 1.0
    for axis_at, shards_of in pieces:
        draws = jax.random.uniform(jax.random.fold_in(jax.random.fold_in(key, 6), axis_at), (shards_of,), jnp.float32, low / len(pieces), top_value / len(pieces))
        loudness = loudness * jnp.repeat(jnp.exp(draws), extent[axis_at] // shards_of).reshape((-1,) + (1,) * (len(extent) - 1 - axis_at))
    return loudness


def bell_draw(rng, dims, width, most, shards=(), held_as=jnp.bfloat16):
    result = width * jax.random.normal(rng, dims, jnp.float32)
    if shards:
        result = result * steps_of(rng, dims, shards, -0.22, 0.18)
    return jnp.clip(result, -most, most).astype(held_as)


def setup_inputs(seed: int = 0) -> dict:
    arg_keys = jax.random.split(jax.random.key(seed), 4)
    lam = bell_draw(arg_keys[0], (NIRREP, OCC_PAIRS, CDH), 1.0, 6.0, ((2, 512),))
    integrals = bell_draw(arg_keys[1], (NIRREP, CDH, ABH), CDH ** -0.5, 0.046875, ((1, 16), (2, 32)))
    block_mask = place_ends((jax.random.randint(arg_keys[2], (NIRREP, CDBLOCKS), 0, 8) < 7).astype(jnp.int32), jax.random.fold_in(arg_keys[2], 1), 0, 1)
    return dict(lam=lam, integrals=integrals, block_mask=block_mask)


def reference(lam, integrals, block_mask):
    def one_irrep(index):
        amplitudes = lam[index]
        weights = integrals[index]
        live = jnp.repeat(block_mask[index], CBH) == 1
        kept = jnp.where(live[:, None], weights, jnp.zeros_like(weights))
        return jnp.dot(amplitudes, kept, preferred_element_type=jnp.float32).astype(jnp.bfloat16)

    return lax.map(one_irrep, jnp.arange(NIRREP, dtype=jnp.int32))
```

```python
import functools

import jax
import jax.numpy as jnp
from jax import lax
from jax.experimental import pallas as pl
from jax.experimental.pallas import tpu as pltpu
from jax.sharding import PartitionSpec as P

MESH = pl.DeviceIdType.MESH
NZ = 8
NY = 8
NQ = 4
F32 = jnp.float32


def kernel(nh, lam, w, mask, out, q_buf, a_buf, w_buf, p_buf, r_buf, x_buf, fx_buf, t_buf, s_buf,
           lam_s, lam_r, lam_l, w_s, w_r, w_l, ag_s, ag_r, rs_s, rs_r, x_s, x_r, t_s, t_r):
    nst = 2 * nh
    ij = lam.shape[2]
    half = ij // 2
    ab = w.shape[2]
    rows = half // NY

    loop = lax.axis_index("loop")
    rep = lax.axis_index("rep")
    z = loop // NQ
    quad = loop % NQ
    core = loop % 2
    x_hi = quad // 2
    x_lo = rep // NY
    y = rep % NY
    first = core * nh
    other = (1 - core) * nh

    def dev(loop_to, rep_to):
        return {"loop": loop_to, "rep": rep_to}

    sibling = dev(z * NQ + x_hi * 2 + (1 - core), rep)
    quads = (
        (sibling, other),
        (dev(z * NQ + (1 - x_hi) * 2 + core, rep), first),
        (dev(z * NQ + (1 - x_hi) * 2 + (1 - core), rep), other),
    )
    z_to = (dev((z + 1) % NZ * NQ + quad, rep), dev((z + NZ - 1) % NZ * NQ + quad, rep))
    y_to = (dev(loop, x_lo * NY + (y + 1) % NY), dev(loop, x_lo * NY + (y + NY - 1) % NY))
    x_to = dev(loop, (1 - x_lo) * NY + y)

    def remote(src, dst, send, recv, to):
        return pltpu.make_async_remote_copy(
            src_ref=src, dst_ref=dst, send_sem=send, recv_sem=recv, device_id=to, device_id_type=MESH)

    def lam_local(i):
        return pltpu.make_async_copy(lam.at[first + i], q_buf.at[i, quad], lam_l.at[i])

    def w_local(i):
        return pltpu.make_async_copy(w.at[first + i], w_buf.at[0, i], w_l.at[i])

    for i in range(nh):
        lam_local(i).start()
    for i in range(nh):
        w_local(i).start()

    barrier = pltpu.get_barrier_semaphore()
    peers = [to for to, _ in quads] + list(z_to) + list(y_to) + [x_to]
    for to in peers:
        pl.semaphore_signal(barrier, inc=1, device_id=to, device_id_type=MESH)
    pl.semaphore_wait(barrier, len(peers))

    def lam_send(d, i):
        to, h0 = quads[d]
        return remote(lam.at[h0 + i], q_buf.at[i, quad], lam_s.at[d, i], lam_r.at[d, i], to)

    def w_send(i):
        return remote(w.at[other + i], w_buf.at[1, i], w_s.at[i], w_r.at[i], sibling)

    for i in range(nh):
        for d in (1, 2, 0):
            lam_send(d, i).start()
    for i in range(nh):
        w_send(i).start()

    def prep(i):
        lam_local(i).wait()
        for d in range(3):
            lam_send(d, i).wait_recv()
        parts = []
        for k in range(NQ):
            live = mask[first + i, z * NQ + k].astype(F32)
            parts.append(q_buf[i, k].astype(F32) * live)
        block = jnp.concatenate(parts, axis=0).T.astype(jnp.bfloat16)
        a_buf[2 * i + (1 - x_lo), z] = block[:half]
        a_buf[2 * i + x_lo, z] = block[half:]

    def ag_hops(d, s):
        return NZ // 2 if d == s % 2 else NZ // 2 - 1

    def ag_from(d, back):
        return (z + NZ - back) % NZ if d == 0 else (z + back) % NZ

    def ag_copy(d, s, k, back):
        block = a_buf.at[s, ag_from(d, back)]
        return remote(block, block, ag_s.at[d, s, k - 1], ag_r.at[d, s, k - 1], z_to[d])

    def ag_start(d, s, k):
        ag_copy(d, s, k, k - 1).start()

    def ag_wait(d, s, k):
        ag_copy(d, s, k, k).wait_recv()

    def rs_hops(d, s):
        return NY // 2 if d == s % 2 else NY // 2 - 1

    def rs_owner(d, m):
        return (y + m) % NY if d == 0 else (y + NY - m) % NY

    def rs_copy(d, s, m):
        src = p_buf.at[s, rs_owner(d, m)] if m == rs_hops(d, s) else r_buf.at[d, s, m]
        return remote(src, r_buf.at[d, s, m - 1], rs_s.at[d, s, m - 1], rs_r.at[d, s, m - 1], y_to[d])

    def rs_arrive(d, s, m):
        rs_copy(d, s, m + 1).wait_recv()
        if m > 0:
            r_buf[d, s, m] = r_buf[d, s, m] + p_buf[s, rs_owner(d, m)]
            rs_copy(d, s, m).start()

    def x_copy(i):
        return remote(fx_buf.at[i], x_buf.at[i], x_s.at[i], x_r.at[i], x_to)

    def t_copy(i):
        return remote(t_buf.at[i], s_buf.at[i], t_s.at[i], t_r.at[i], sibling)

    def matmul(s):
        i = s // 2
        if s % 2 == 0:
            w_local(i).wait()
            w_send(i).wait_recv()
        block = jnp.concatenate([a_buf[s, k] for k in range(NZ)], axis=1)
        for side in range(2):
            part = jnp.dot(block, w_buf[side, i], preferred_element_type=F32)
            p_buf[s, :, :, side * ab:(side + 1) * ab] = part.reshape(NY, rows, ab)

    def final(s):
        i = s // 2
        total = p_buf[s, y] + r_buf[0, s, 0] + r_buf[1, s, 0]
        if s % 2 == 0:
            fx_buf[i] = total
            x_copy(i).start()
        else:
            x_copy(i).wait_recv()
            done = (total + x_buf[i]).astype(jnp.bfloat16)
            out[first + i] = done[:, :ab]
            t_buf[i] = done[:, ab:]
            t_copy(i).start()

    def phase(s, p):
        if p == 0:
            if s % 2 == 0:
                prep(s // 2)
            for d in range(2):
                ag_start(d, s, 1)
        elif p <= 4:
            for d in range(2):
                if p <= ag_hops(d, s):
                    ag_wait(d, s, p)
                    if p < ag_hops(d, s):
                        ag_start(d, s, p + 1)
            if p == 4:
                matmul(s)
                for d in range(2):
                    rs_copy(d, s, rs_hops(d, s)).start()
        else:
            for d in range(2):
                m = rs_hops(d, s) - (p - 4)
                if m >= 0:
                    rs_arrive(d, s, m)
            if p == 8:
                final(s)

    for tick in range(nst + 8):
        for p in (3, 7, 2, 6, 1, 5, 0, 4, 8):
            if 0 <= tick - p < nst:
                phase(tick - p, p)

    for i in range(nh):
        t_copy(i).wait_recv()
        out[other + i] = s_buf[i]

    for i in range(nh):
        for d in range(3):
            lam_send(d, i).wait_send()
        w_send(i).wait_send()
        x_copy(i).wait_send()
        t_copy(i).wait_send()
    for s in range(nst):
        for d in range(2):
            for k in range(1, ag_hops(d, s) + 1):
                ag_copy(d, s, k, k - 1).wait_send()
            for m in range(1, rs_hops(d, s) + 1):
                rs_copy(d, s, m).wait_send()


def per_device(lam, integrals, block_mask):
    nirrep, ij, cb = lam.shape
    _, cd, ab = integrals.shape
    nh = nirrep // 2
    nst = 2 * nh
    half = ij // 2
    rows = half // NY
    bf = jnp.bfloat16
    dma = pltpu.SemaphoreType.DMA
    any_spec = pl.BlockSpec(memory_space=pl.ANY)
    return pl.pallas_call(
        functools.partial(kernel, nh),
        out_shape=jax.ShapeDtypeStruct((nirrep, rows, ab), bf),
        in_specs=[any_spec, any_spec, pl.BlockSpec(memory_space=pltpu.SMEM)],
        out_specs=pl.BlockSpec(memory_space=pltpu.VMEM),
        scratch_shapes=[
            pltpu.VMEM((nh, NQ, cb, ij), bf),
            pltpu.VMEM((nst, NZ, half, NQ * cb), bf),
            pltpu.VMEM((2, nh, cd, ab), bf),
            pltpu.VMEM((nst, NY, rows, 2 * ab), F32),
            pltpu.VMEM((2, nst, 4, rows, 2 * ab), F32),
            pltpu.VMEM((nh, rows, 2 * ab), F32),
            pltpu.VMEM((nh, rows, 2 * ab), F32),
            pltpu.VMEM((nh, rows, ab), bf),
            pltpu.VMEM((nh, rows, ab), bf),
            dma((3, nh)), dma((3, nh)), dma((nh,)),
            dma((nh,)), dma((nh,)), dma((nh,)),
            dma((2, nst, 4)), dma((2, nst, 4)),
            dma((2, nst, 4)), dma((2, nst, 4)),
            dma((nh,)), dma((nh,)),
            dma((nh,)), dma((nh,)),
        ],
        compiler_params=pltpu.CompilerParams(collective_id=0, has_side_effects=True),
    )(lam.transpose(0, 2, 1), integrals, block_mask)


def solution(mesh):
    return jax.shard_map(
        per_device,
        mesh=mesh,
        in_specs=(P(None, None, ("rep", "loop")), P(None, "rep", "loop"), P(None, "rep")),
        out_specs=P(None, "rep", "loop"),
        check_vma=False,
    )
```

```python
import functools

import jax
import jax.numpy as jnp
from jax import lax
from jax.experimental import pallas as pl
from jax.experimental.pallas import tpu as pltpu
from jax.sharding import PartitionSpec as P

MESH = pl.DeviceIdType.MESH
NZ = 8
NY = 8
NQ = 4
F32 = jnp.float32
I16 = jnp.int16
SCALE_ROWS = 16


def encode(v):
    top = jnp.maximum(jnp.max(jnp.abs(v), axis=0, keepdims=True), 1e-37)
    c = jnp.maximum(jnp.ceil(jnp.log2(top)) - 15, -126)
    q = jnp.clip(jnp.round(v * jnp.exp2(-c)), -32767, 32767)
    coded = jnp.concatenate([q, jnp.broadcast_to(c, (SCALE_ROWS, v.shape[1]))], axis=0)
    return coded.astype(jnp.int32).astype(I16)


def decode(coded):
    f = coded.astype(jnp.int32).astype(F32)
    rows = f.shape[0] - SCALE_ROWS
    return f[:rows] * jnp.exp2(f[rows:rows + 1])


def kernel(nh, lam, w, mask, out, q_buf, a_buf, w_buf, p_buf, e_buf, r_buf, x_buf, fx_buf, t_buf, s_buf,
           lam_s, lam_r, lam_l, w_s, w_r, w_l, ag_s, ag_r, rs_s, rs_r, x_s, x_r, t_s, t_r):
    nst = 2 * nh
    ij = lam.shape[2]
    half = ij // 2
    ab = w.shape[2]
    rows = half // NY

    loop = lax.axis_index("loop")
    rep = lax.axis_index("rep")
    z = loop // NQ
    quad = loop % NQ
    core = loop % 2
    x_hi = quad // 2
    x_lo = rep // NY
    y = rep % NY
    first = core * nh
    other = (1 - core) * nh

    def dev(loop_to, rep_to):
        return {"loop": loop_to, "rep": rep_to}

    sibling = dev(z * NQ + x_hi * 2 + (1 - core), rep)
    quads = (
        (sibling, other),
        (dev(z * NQ + (1 - x_hi) * 2 + core, rep), first),
        (dev(z * NQ + (1 - x_hi) * 2 + (1 - core), rep), other),
    )
    z_to = (dev((z + 1) % NZ * NQ + quad, rep), dev((z + NZ - 1) % NZ * NQ + quad, rep))
    y_to = (dev(loop, x_lo * NY + (y + 1) % NY), dev(loop, x_lo * NY + (y + NY - 1) % NY))
    x_to = dev(loop, (1 - x_lo) * NY + y)

    def remote(src, dst, send, recv, to):
        return pltpu.make_async_remote_copy(
            src_ref=src, dst_ref=dst, send_sem=send, recv_sem=recv, device_id=to, device_id_type=MESH)

    def lam_local(i):
        return pltpu.make_async_copy(lam.at[first + i], q_buf.at[i, quad], lam_l.at[i])

    def w_local(i):
        return pltpu.make_async_copy(w.at[first + i], w_buf.at[0, i], w_l.at[i])

    for i in range(nh):
        lam_local(i).start()
    for i in range(nh):
        w_local(i).start()

    barrier = pltpu.get_barrier_semaphore()
    peers = [to for to, _ in quads] + list(z_to) + list(y_to) + [x_to]
    for to in peers:
        pl.semaphore_signal(barrier, inc=1, device_id=to, device_id_type=MESH)
    pl.semaphore_wait(barrier, len(peers))

    def lam_send(d, i):
        to, h0 = quads[d]
        return remote(lam.at[h0 + i], q_buf.at[i, quad], lam_s.at[d, i], lam_r.at[d, i], to)

    def w_send(i):
        return remote(w.at[other + i], w_buf.at[1, i], w_s.at[i], w_r.at[i], sibling)

    for i in range(nh):
        for d in (1, 2, 0):
            lam_send(d, i).start()
    for i in range(nh):
        w_send(i).start()

    def prep(i):
        lam_local(i).wait()
        for d in range(3):
            lam_send(d, i).wait_recv()
        parts = []
        for k in range(NQ):
            live = mask[first + i, z * NQ + k].astype(F32)
            parts.append(q_buf[i, k].astype(F32) * live)
        block = jnp.concatenate(parts, axis=0).T.astype(jnp.bfloat16)
        a_buf[2 * i + (1 - x_lo), z] = block[:half]
        a_buf[2 * i + x_lo, z] = block[half:]

    def ag_hops(d, s):
        return NZ // 2 if d == s % 2 else NZ // 2 - 1

    def ag_from(d, back):
        return (z + NZ - back) % NZ if d == 0 else (z + back) % NZ

    def ag_copy(d, s, k, back):
        block = a_buf.at[s, ag_from(d, back)]
        return remote(block, block, ag_s.at[d, s, k - 1], ag_r.at[d, s, k - 1], z_to[d])

    def ag_start(d, s, k):
        ag_copy(d, s, k, k - 1).start()

    def ag_wait(d, s, k):
        ag_copy(d, s, k, k).wait_recv()

    def rs_hops(d, s):
        return NY // 2 if d == s % 2 else NY // 2 - 1

    def rs_owner(d, m):
        return (y + m) % NY if d == 0 else (y + NY - m) % NY

    def rs_copy(d, s, m):
        return remote(e_buf.at[d, s, m - 1], r_buf.at[d, s, m - 1], rs_s.at[d, s, m - 1], rs_r.at[d, s, m - 1], y_to[d])

    def rs_start(d, s):
        m = rs_hops(d, s)
        e_buf[d, s, m - 1] = encode(p_buf[s, rs_owner(d, m)])
        rs_copy(d, s, m).start()

    def rs_arrive(d, s, m):
        rs_copy(d, s, m + 1).wait_recv()
        if m > 0:
            e_buf[d, s, m - 1] = encode(decode(r_buf[d, s, m]) + p_buf[s, rs_owner(d, m)])
            rs_copy(d, s, m).start()

    def x_copy(i):
        return remote(fx_buf.at[i], x_buf.at[i], x_s.at[i], x_r.at[i], x_to)

    def t_copy(i):
        return remote(t_buf.at[i], s_buf.at[i], t_s.at[i], t_r.at[i], sibling)

    def matmul(s):
        i = s // 2
        if s % 2 == 0:
            w_local(i).wait()
            w_send(i).wait_recv()
        block = jnp.concatenate([a_buf[s, k] for k in range(NZ)], axis=1)
        for side in range(2):
            part = jnp.dot(block, w_buf[side, i], preferred_element_type=F32)
            p_buf[s, :, side * rows:(side + 1) * rows] = part.reshape(NY, rows, ab)

    def final(s):
        i = s // 2
        total = p_buf[s, y] + decode(r_buf[0, s, 0]) + decode(r_buf[1, s, 0])
        if s % 2 == 0:
            fx_buf[i] = total
            x_copy(i).start()
        else:
            x_copy(i).wait_recv()
            done = (total + x_buf[i]).astype(jnp.bfloat16)
            out[first + i] = done[:rows]
            t_buf[i] = done[rows:]
            t_copy(i).start()

    def phase(s, p):
        if p == 0:
            if s % 2 == 0:
                prep(s // 2)
            for d in range(2):
                ag_start(d, s, 1)
        elif p <= 4:
            for d in range(2):
                if p <= ag_hops(d, s):
                    ag_wait(d, s, p)
                    if p < ag_hops(d, s):
                        ag_start(d, s, p + 1)
            if p == 4:
                matmul(s)
                for d in range(2):
                    rs_start(d, s)
        else:
            for d in range(2):
                m = rs_hops(d, s) - (p - 4)
                if m >= 0:
                    rs_arrive(d, s, m)
            if p == 8:
                final(s)

    for tick in range(nst + 8):
        for p in (3, 7, 2, 6, 1, 5, 0, 4, 8):
            if 0 <= tick - p < nst:
                phase(tick - p, p)

    for i in range(nh):
        t_copy(i).wait_recv()
        out[other + i] = s_buf[i]

    for i in range(nh):
        for d in range(3):
            lam_send(d, i).wait_send()
        w_send(i).wait_send()
        x_copy(i).wait_send()
        t_copy(i).wait_send()
    for s in range(nst):
        for d in range(2):
            for k in range(1, ag_hops(d, s) + 1):
                ag_copy(d, s, k, k - 1).wait_send()
            for m in range(1, rs_hops(d, s) + 1):
                rs_copy(d, s, m).wait_send()


def per_device(lam, integrals, block_mask):
    nirrep, ij, cb = lam.shape
    _, cd, ab = integrals.shape
    nh = nirrep // 2
    nst = 2 * nh
    half = ij // 2
    rows = half // NY
    bf = jnp.bfloat16
    dma = pltpu.SemaphoreType.DMA
    any_spec = pl.BlockSpec(memory_space=pl.ANY)
    return pl.pallas_call(
        functools.partial(kernel, nh),
        out_shape=jax.ShapeDtypeStruct((nirrep, rows, ab), bf),
        in_specs=[any_spec, any_spec, pl.BlockSpec(memory_space=pltpu.SMEM)],
        out_specs=pl.BlockSpec(memory_space=pltpu.VMEM),
        scratch_shapes=[
            pltpu.VMEM((nh, NQ, cb, ij), bf),
            pltpu.VMEM((nst, NZ, half, NQ * cb), bf),
            pltpu.VMEM((2, nh, cd, ab), bf),
            pltpu.VMEM((nst, NY, 2 * rows, ab), F32),
            pltpu.VMEM((2, nst, 4, 2 * rows + SCALE_ROWS, ab), I16),
            pltpu.VMEM((2, nst, 4, 2 * rows + SCALE_ROWS, ab), I16),
            pltpu.VMEM((nh, 2 * rows, ab), F32),
            pltpu.VMEM((nh, 2 * rows, ab), F32),
            pltpu.VMEM((nh, rows, ab), bf),
            pltpu.VMEM((nh, rows, ab), bf),
            dma((3, nh)), dma((3, nh)), dma((nh,)),
            dma((nh,)), dma((nh,)), dma((nh,)),
            dma((2, nst, 4)), dma((2, nst, 4)),
            dma((2, nst, 4)), dma((2, nst, 4)),
            dma((nh,)), dma((nh,)),
            dma((nh,)), dma((nh,)),
        ],
        compiler_params=pltpu.CompilerParams(collective_id=0, has_side_effects=True),
    )(lam.transpose(0, 2, 1), integrals, block_mask)


def solution(mesh):
    return jax.shard_map(
        per_device,
        mesh=mesh,
        in_specs=(P(None, None, ("rep", "loop")), P(None, "rep", "loop"), P(None, "rep")),
        out_specs=P(None, "rep", "loop"),
        check_vma=False,
    )
```

```python
import functools

import jax
import jax.numpy as jnp
from jax import lax
from jax.experimental import pallas as pl
from jax.experimental.pallas import tpu as pltpu
from jax.sharding import PartitionSpec as P

MESH = pl.DeviceIdType.MESH
NZ = 8
NY = 8
NQ = 4
F32 = jnp.float32
I16 = jnp.int16
SCALE_ROWS = 16

ORDER = (
    (0, 0), (1, 0), (1, 1), (0, 1), (1, 2), (1, 3), (0, 2), (0, 3), (2, 0, 0, 1), (2, 1, 0, 1), (2, 0, 1, 1),
    (2, 1, 1, 1), (2, 0, 2, 1), (2, 1, 2, 1), (2, 0, 3, 1), (2, 1, 3, 1), (2, 0, 0, 2), (2, 1, 0, 2),
    (2, 0, 1, 2), (2, 1, 1, 2), (2, 0, 2, 2), (2, 1, 2, 2), (2, 0, 3, 2), (2, 1, 3, 2), (2, 0, 0, 3),
    (2, 1, 0, 3), (1, 4), (2, 0, 1, 3), (2, 1, 1, 3), (1, 5), (2, 0, 2, 3), (2, 1, 2, 3), (1, 6),
    (2, 0, 3, 3), (2, 1, 3, 3), (1, 7), (2, 1, 4, 1), (2, 0, 0, 4), (3, 0), (2, 1, 1, 4), (3, 1),
    (2, 0, 4, 1), (2, 0, 5, 1), (2, 1, 5, 1), (2, 1, 6, 1), (2, 0, 2, 4), (3, 2), (4, 0, 0, 1), (4, 1, 0, 1),
    (2, 0, 6, 1), (2, 1, 3, 4), (3, 3), (2, 0, 7, 1), (2, 1, 7, 1), (4, 0, 1, 1), (4, 1, 1, 1), (2, 0, 4, 2),
    (2, 1, 4, 2), (4, 0, 2, 1), (4, 1, 2, 1), (2, 0, 5, 2), (2, 1, 5, 2), (4, 0, 0, 2), (4, 1, 0, 2),
    (4, 0, 3, 1), (2, 0, 6, 2), (2, 1, 6, 2), (4, 1, 3, 1), (4, 0, 1, 2), (4, 1, 1, 2), (2, 0, 7, 2),
    (2, 1, 7, 2), (4, 0, 2, 2), (4, 1, 2, 2), (2, 0, 4, 3), (2, 1, 4, 3), (4, 0, 0, 3), (4, 1, 0, 3),
    (2, 0, 5, 3), (2, 1, 5, 3), (4, 0, 3, 2), (4, 1, 3, 2), (4, 0, 1, 3), (2, 0, 6, 3), (2, 1, 6, 3),
    (4, 1, 1, 3), (4, 0, 2, 3), (4, 1, 2, 3), (2, 0, 7, 3), (2, 1, 7, 3), (4, 0, 0, 4), (5, 0), (2, 0, 4, 4),
    (3, 4), (4, 0, 3, 3), (4, 1, 3, 3), (4, 1, 1, 4), (2, 0, 6, 4), (3, 6), (2, 1, 5, 4), (3, 5),
    (2, 1, 7, 4), (3, 7), (4, 0, 4, 1), (4, 1, 4, 1), (4, 1, 3, 4), (5, 1), (4, 0, 6, 1), (4, 0, 2, 4),
    (5, 2), (4, 1, 6, 1), (4, 0, 5, 1), (4, 1, 5, 1), (4, 0, 7, 1), (4, 1, 7, 1), (4, 0, 4, 2), (4, 1, 4, 2),
    (4, 0, 6, 2), (4, 1, 6, 2), (5, 3), (4, 0, 5, 2), (4, 1, 5, 2), (4, 0, 7, 2), (4, 1, 7, 2), (4, 0, 4, 3),
    (4, 1, 4, 3), (4, 0, 6, 3), (4, 1, 6, 3), (4, 0, 5, 3), (4, 1, 5, 3), (4, 0, 7, 3), (4, 1, 7, 3),
    (4, 0, 4, 4), (5, 4), (4, 0, 6, 4), (5, 6), (4, 1, 5, 4), (4, 1, 7, 4), (5, 5), (5, 7),
)


def encode(v):
    top = jnp.maximum(jnp.max(jnp.abs(v), axis=0, keepdims=True), 1e-37)
    c = jnp.maximum(jnp.ceil(jnp.log2(top)) - 15, -126)
    q = jnp.clip(jnp.round(v * jnp.exp2(-c)), -32767, 32767)
    coded = jnp.concatenate([q, jnp.broadcast_to(c, (SCALE_ROWS, v.shape[1]))], axis=0)
    return coded.astype(jnp.int32).astype(I16)


def decode(coded):
    f = coded.astype(jnp.int32).astype(F32)
    rows = f.shape[0] - SCALE_ROWS
    return f[:rows] * jnp.exp2(f[rows:rows + 1])


def kernel(nh, lam, w, mask, out, q_buf, a_buf, w_buf, p_buf, e_buf, r_buf, x_buf, fx_buf, t_buf, s_buf,
           lam_s, lam_r, lam_l, w_s, w_r, w_l, ag_s, ag_r, rs_s, rs_r, x_s, x_r, t_s, t_r):
    nst = 2 * nh
    ij = lam.shape[2]
    half = ij // 2
    ab = w.shape[2]
    rows = half // NY

    loop = lax.axis_index("loop")
    rep = lax.axis_index("rep")
    z = loop // NQ
    quad = loop % NQ
    core = loop % 2
    x_hi = quad // 2
    x_lo = rep // NY
    y = rep % NY
    first = core * nh
    other = (1 - core) * nh

    def dev(loop_to, rep_to):
        return {"loop": loop_to, "rep": rep_to}

    sibling = dev(z * NQ + x_hi * 2 + (1 - core), rep)
    quads = (
        (sibling, other),
        (dev(z * NQ + (1 - x_hi) * 2 + core, rep), first),
        (dev(z * NQ + (1 - x_hi) * 2 + (1 - core), rep), other),
    )
    z_to = (dev((z + 1) % NZ * NQ + quad, rep), dev((z + NZ - 1) % NZ * NQ + quad, rep))
    y_to = (dev(loop, x_lo * NY + (y + 1) % NY), dev(loop, x_lo * NY + (y + NY - 1) % NY))
    x_to = dev(loop, (1 - x_lo) * NY + y)

    def remote(src, dst, send, recv, to):
        return pltpu.make_async_remote_copy(
            src_ref=src, dst_ref=dst, send_sem=send, recv_sem=recv, device_id=to, device_id_type=MESH)

    def lam_local(i):
        return pltpu.make_async_copy(lam.at[first + i], q_buf.at[i, quad], lam_l.at[i])

    def w_local(i):
        return pltpu.make_async_copy(w.at[first + i], w_buf.at[0, i], w_l.at[i])

    for i in range(nh):
        lam_local(i).start()
    for i in range(nh):
        w_local(i).start()

    barrier = pltpu.get_barrier_semaphore()
    peers = [to for to, _ in quads] + list(z_to) + list(y_to) + [x_to]
    for to in peers:
        pl.semaphore_signal(barrier, inc=1, device_id=to, device_id_type=MESH)
    pl.semaphore_wait(barrier, len(peers))

    def lam_send(d, i):
        to, h0 = quads[d]
        return remote(lam.at[h0 + i], q_buf.at[i, quad], lam_s.at[d, i], lam_r.at[d, i], to)

    def w_send(i):
        return remote(w.at[other + i], w_buf.at[1, i], w_s.at[i], w_r.at[i], sibling)

    for i in range(nh):
        for d in (1, 2, 0):
            lam_send(d, i).start()
    for i in range(nh):
        w_send(i).start()

    def prep(i):
        lam_local(i).wait()
        for d in range(3):
            lam_send(d, i).wait_recv()
        parts = []
        for k in range(NQ):
            live = mask[first + i, z * NQ + k].astype(F32)
            parts.append(q_buf[i, k].astype(F32) * live)
        block = jnp.concatenate(parts, axis=0).T.astype(jnp.bfloat16)
        a_buf[2 * i + (1 - x_lo), z] = block[:half]
        a_buf[2 * i + x_lo, z] = block[half:]

    def ag_hops(d, s):
        return NZ // 2 if d == s % 2 else NZ // 2 - 1

    def ag_from(d, back):
        return (z + NZ - back) % NZ if d == 0 else (z + back) % NZ

    def ag_copy(d, s, k, back):
        block = a_buf.at[s, ag_from(d, back)]
        return remote(block, block, ag_s.at[d, s, k - 1], ag_r.at[d, s, k - 1], z_to[d])

    def ag_start(d, s, k):
        ag_copy(d, s, k, k - 1).start()

    def ag_wait(d, s, k):
        ag_copy(d, s, k, k).wait_recv()

    def rs_hops(d, s):
        return NY // 2 if d == s % 2 else NY // 2 - 1

    def rs_owner(d, m):
        return (y + m) % NY if d == 0 else (y + NY - m) % NY

    def rs_copy(d, s, m):
        return remote(e_buf.at[d, s, m - 1], r_buf.at[d, s, m - 1], rs_s.at[d, s, m - 1], rs_r.at[d, s, m - 1], y_to[d])

    def rs_start(d, s):
        m = rs_hops(d, s)
        e_buf[d, s, m - 1] = encode(p_buf[s, rs_owner(d, m)])
        rs_copy(d, s, m).start()

    def rs_arrive(d, s, m):
        rs_copy(d, s, m + 1).wait_recv()
        if m > 0:
            e_buf[d, s, m - 1] = encode(decode(r_buf[d, s, m]) + p_buf[s, rs_owner(d, m)])
            rs_copy(d, s, m).start()

    def x_copy(i):
        return remote(fx_buf.at[i], x_buf.at[i], x_s.at[i], x_r.at[i], x_to)

    def t_copy(i):
        return remote(t_buf.at[i], s_buf.at[i], t_s.at[i], t_r.at[i], sibling)

    def matmul(s):
        i = s // 2
        if s % 2 == 0:
            w_local(i).wait()
            w_send(i).wait_recv()
        block = jnp.concatenate([a_buf[s, k] for k in range(NZ)], axis=1)
        for side in range(2):
            part = jnp.dot(block, w_buf[side, i], preferred_element_type=F32)
            p_buf[s, :, side * rows:(side + 1) * rows] = part.reshape(NY, rows, ab)

    def final(s):
        i = s // 2
        total = p_buf[s, y] + decode(r_buf[0, s, 0]) + decode(r_buf[1, s, 0])
        if s % 2 == 0:
            fx_buf[i] = total
            x_copy(i).start()
        else:
            x_copy(i).wait_recv()
            done = (total + x_buf[i]).astype(jnp.bfloat16)
            out[first + i] = done[:rows]
            t_buf[i] = done[rows:]
            t_copy(i).start()

    def gather_step(d, s, k):
        ag_wait(d, s, k)
        if k < ag_hops(d, s):
            ag_start(d, s, k + 1)

    def gather_first(s):
        for d in range(2):
            ag_start(d, s, 1)

    def multiply(s):
        matmul(s)
        for d in range(2):
            rs_start(d, s)

    def sum_step(d, s, k):
        rs_arrive(d, s, rs_hops(d, s) - k)

    steps = (prep, gather_first, gather_step, multiply, sum_step, final)
    for kind, *which in ORDER:
        steps[kind](*which)

    for i in range(nh):
        t_copy(i).wait_recv()
        out[other + i] = s_buf[i]

    for i in range(nh):
        for d in range(3):
            lam_send(d, i).wait_send()
        w_send(i).wait_send()
        x_copy(i).wait_send()
        t_copy(i).wait_send()
    for s in range(nst):
        for d in range(2):
            for k in range(1, ag_hops(d, s) + 1):
                ag_copy(d, s, k, k - 1).wait_send()
            for m in range(1, rs_hops(d, s) + 1):
                rs_copy(d, s, m).wait_send()


def per_device(lam, integrals, block_mask):
    nirrep, ij, cb = lam.shape
    _, cd, ab = integrals.shape
    nh = nirrep // 2
    nst = 2 * nh
    half = ij // 2
    rows = half // NY
    bf = jnp.bfloat16
    dma = pltpu.SemaphoreType.DMA
    any_spec = pl.BlockSpec(memory_space=pl.ANY)
    return pl.pallas_call(
        functools.partial(kernel, nh),
        out_shape=jax.ShapeDtypeStruct((nirrep, rows, ab), bf),
        in_specs=[any_spec, any_spec, pl.BlockSpec(memory_space=pltpu.SMEM)],
        out_specs=pl.BlockSpec(memory_space=pltpu.VMEM),
        scratch_shapes=[
            pltpu.VMEM((nh, NQ, cb, ij), bf),
            pltpu.VMEM((nst, NZ, half, NQ * cb), bf),
            pltpu.VMEM((2, nh, cd, ab), bf),
            pltpu.VMEM((nst, NY, 2 * rows, ab), F32),
            pltpu.VMEM((2, nst, 4, 2 * rows + SCALE_ROWS, ab), I16),
            pltpu.VMEM((2, nst, 4, 2 * rows + SCALE_ROWS, ab), I16),
            pltpu.VMEM((nh, 2 * rows, ab), F32),
            pltpu.VMEM((nh, 2 * rows, ab), F32),
            pltpu.VMEM((nh, rows, ab), bf),
            pltpu.VMEM((nh, rows, ab), bf),
            dma((3, nh)), dma((3, nh)), dma((nh,)),
            dma((nh,)), dma((nh,)), dma((nh,)),
            dma((2, nst, 4)), dma((2, nst, 4)),
            dma((2, nst, 4)), dma((2, nst, 4)),
            dma((nh,)), dma((nh,)),
            dma((nh,)), dma((nh,)),
        ],
        compiler_params=pltpu.CompilerParams(collective_id=0, has_side_effects=True),
    )(lam.transpose(0, 2, 1), integrals, block_mask)


def solution(mesh):
    return jax.shard_map(
        per_device,
        mesh=mesh,
        in_specs=(P(None, None, ("rep", "loop")), P(None, "rep", "loop"), P(None, "rep")),
        out_specs=P(None, "rep", "loop"),
        check_vma=False,
    )
```

```python
import functools

import jax
import jax.numpy as jnp
from jax import lax
from jax.experimental import pallas as pl
from jax.experimental.pallas import tpu as pltpu
from jax.sharding import PartitionSpec as P

MESH = pl.DeviceIdType.MESH
NZ = 8
NY = 8
NF = 2
NQ = 4
F32 = jnp.float32
I16 = jnp.int16
SCALE_ROWS = 16

ORDER = (
    (0, 0), (1, 0), (0, 1), (1, 2), (0, 2), (1, 4), (2, 1, 0, 1), (2, 0, 0, 1), (1, 5), (2, 1, 2, 1), (0, 3),
    (1, 6), (2, 0, 2, 1), (2, 1, 0, 2), (2, 0, 0, 2), (1, 7), (2, 0, 6, 1), (2, 1, 2, 2), (2, 0, 2, 2),
    (2, 1, 0, 3), (2, 1, 4, 1), (2, 0, 0, 3), (2, 0, 4, 1), (2, 1, 6, 1), (2, 1, 2, 3), (2, 1, 7, 1),
    (2, 0, 6, 2), (2, 1, 4, 2), (2, 0, 7, 1), (2, 0, 0, 4), (2, 0, 2, 3), (2, 1, 5, 1), (2, 0, 4, 2),
    (2, 1, 2, 4), (2, 1, 7, 2), (2, 0, 5, 1), (6, 0), (2, 0, 6, 3), (2, 1, 6, 2), (3, 0), (3, 1),
    (2, 0, 4, 3), (2, 1, 5, 2), (6, 1), (2, 0, 7, 2), (3, 3), (3, 2), (4, 0, 0, 1), (2, 1, 6, 3),
    (2, 0, 6, 4), (2, 1, 7, 3), (2, 0, 5, 2), (4, 1, 0, 1), (2, 1, 4, 3), (3, 6), (4, 0, 1, 1), (2, 1, 5, 3),
    (4, 1, 1, 1), (2, 0, 4, 4), (3, 4), (4, 0, 2, 1), (4, 1, 3, 1), (4, 1, 0, 2), (2, 0, 7, 3), (4, 0, 0, 2),
    (2, 0, 5, 3), (2, 1, 7, 4), (4, 1, 2, 1), (4, 0, 6, 1), (3, 7), (4, 0, 4, 1), (2, 1, 5, 4), (4, 1, 6, 1),
    (3, 5), (4, 0, 2, 2), (4, 1, 4, 1), (4, 0, 3, 1), (4, 1, 3, 2), (4, 0, 6, 2), (4, 0, 0, 3), (4, 1, 0, 3),
    (4, 1, 7, 1), (4, 1, 2, 2), (4, 0, 4, 2), (4, 1, 5, 1), (4, 0, 2, 3), (4, 1, 1, 2), (4, 0, 7, 1),
    (4, 1, 6, 2), (4, 0, 6, 3), (4, 1, 7, 2), (4, 0, 5, 1), (4, 0, 0, 4), (5, 0), (4, 1, 4, 2), (4, 1, 2, 3),
    (4, 0, 4, 3), (4, 1, 5, 2), (4, 0, 1, 2), (4, 0, 2, 4), (5, 2), (4, 0, 3, 2), (4, 1, 1, 3), (4, 1, 3, 3),
    (4, 0, 6, 4), (4, 1, 6, 3), (5, 6), (4, 0, 7, 2), (4, 1, 7, 3), (4, 0, 5, 2), (4, 1, 4, 3), (4, 0, 4, 4),
    (5, 4), (4, 1, 5, 3), (4, 0, 3, 3), (4, 1, 7, 4), (4, 1, 3, 4), (4, 0, 1, 3), (5, 3), (4, 1, 1, 4),
    (4, 0, 7, 3), (5, 1), (4, 0, 5, 3), (5, 7), (4, 1, 5, 4), (5, 5),
)


def encode(v):
    top = jnp.maximum(jnp.max(jnp.abs(v), axis=0, keepdims=True), 1e-37)
    c = jnp.maximum(jnp.ceil(jnp.log2(top)) - 15, -126)
    q = jnp.clip(jnp.round(v * jnp.exp2(-c)), -32767, 32767)
    coded = jnp.concatenate([q, jnp.broadcast_to(c, (SCALE_ROWS, v.shape[1]))], axis=0)
    return coded.astype(jnp.int32).astype(I16)


def decode(coded):
    f = coded.astype(jnp.int32).astype(F32)
    rows = f.shape[0] - SCALE_ROWS
    return f[:rows] * jnp.exp2(f[rows:rows + 1])


def kernel(nh, lam, w, mask, out, q_buf, a_buf, w_buf, p_buf, e_buf, r_buf, x_buf, fx_buf, t_buf, s_buf,
           lam_s, lam_r, lam_l, w_s, w_r, w_l, ag_s, ag_r, xg_s, xg_r, rs_s, rs_r, x_s, x_r, t_s, t_r):
    nst = 2 * nh
    ij = lam.shape[2]
    half = ij // 2
    ab = w.shape[2]
    rows = half // NY

    loop = lax.axis_index("loop")
    rep = lax.axis_index("rep")
    z = loop // NQ
    quad = loop % NQ
    core = loop % 2
    x_hi = quad // 2
    x_lo = rep // NY
    y = rep % NY
    first = core * nh
    other = (1 - core) * nh

    def dev(loop_to, rep_to):
        return {"loop": loop_to, "rep": rep_to}

    sibling = dev(z * NQ + x_hi * 2 + (1 - core), rep)
    quads = (
        (sibling, other),
        (dev(z * NQ + (1 - x_hi) * 2 + core, rep), first),
        (dev(z * NQ + (1 - x_hi) * 2 + (1 - core), rep), other),
    )
    z_to = (dev((z + 1) % NZ * NQ + quad, rep), dev((z + NZ - 1) % NZ * NQ + quad, rep))
    y_to = (dev(loop, x_lo * NY + (y + 1) % NY), dev(loop, x_lo * NY + (y + NY - 1) % NY))
    x_to = dev(loop, (1 - x_lo) * NY + y)

    def remote(src, dst, send, recv, to):
        return pltpu.make_async_remote_copy(
            src_ref=src, dst_ref=dst, send_sem=send, recv_sem=recv, device_id=to, device_id_type=MESH)

    def lam_local(i):
        return pltpu.make_async_copy(lam.at[first + i], q_buf.at[i, quad], lam_l.at[i])

    def w_local(i):
        return pltpu.make_async_copy(w.at[first + i], w_buf.at[0, i], w_l.at[i])

    for i in range(nh):
        lam_local(i).start()
    for i in range(nh):
        w_local(i).start()

    barrier = pltpu.get_barrier_semaphore()
    peers = [to for to, _ in quads] + list(z_to) + list(y_to) + [x_to]
    for to in peers:
        pl.semaphore_signal(barrier, inc=1, device_id=to, device_id_type=MESH)
    pl.semaphore_wait(barrier, len(peers))

    def lam_send(d, i):
        to, h0 = quads[d]
        return remote(lam.at[h0 + i], q_buf.at[i, quad], lam_s.at[d, i], lam_r.at[d, i], to)

    def w_send(i):
        return remote(w.at[other + i], w_buf.at[1, i], w_s.at[i], w_r.at[i], sibling)

    for i in range(nh):
        for d in (1, 2, 0):
            lam_send(d, i).start()
    for i in range(nh):
        w_send(i).start()

    def prep(i):
        lam_local(i).wait()
        for d in range(3):
            lam_send(d, i).wait_recv()
        parts = []
        for k in range(NQ):
            live = mask[first + i, z * NQ + k].astype(F32)
            parts.append(q_buf[i, k].astype(F32) * live)
        block = jnp.concatenate(parts, axis=0).T.astype(jnp.bfloat16)
        a_buf[2 * i + (1 - x_lo), z] = block[:half]
        a_buf[2 * i + x_lo, z] = block[half:]

    def ag_hops(d, s):
        return NZ // 2 if d == (s // 2 if s < 2 * NF else s) % 2 else NZ // 2 - 1

    def ag_from(d, back):
        return (z + NZ - back) % NZ if d == 0 else (z + back) % NZ

    def ag_copy(d, s, k, back):
        block = a_buf.at[s + x_hi if s < 2 * NF else s, ag_from(d, back)]
        return remote(block, block, ag_s.at[d, s, k - 1], ag_r.at[d, s, k - 1], z_to[d])

    def ag_start(d, s, k):
        ag_copy(d, s, k, k - 1).start()

    def ag_wait(d, s, k):
        ag_copy(d, s, k, k).wait_recv()

    def xg_copy(d, s, k, side):
        block = a_buf.at[s + side, ag_from(d, k)]
        return remote(block, block, xg_s.at[d, s // 2, k - 1], xg_r.at[d, s // 2, k - 1], quads[1][0])

    def rs_hops(d, s):
        return NY // 2 if d == s % 2 else NY // 2 - 1

    def rs_owner(d, m):
        return (y + m) % NY if d == 0 else (y + NY - m) % NY

    def rs_copy(d, s, m):
        return remote(e_buf.at[d, s, m - 1], r_buf.at[d, s, m - 1], rs_s.at[d, s, m - 1], rs_r.at[d, s, m - 1], y_to[d])

    def rs_start(d, s):
        m = rs_hops(d, s)
        e_buf[d, s, m - 1] = encode(p_buf[s, rs_owner(d, m)])
        rs_copy(d, s, m).start()

    def rs_arrive(d, s, m):
        rs_copy(d, s, m + 1).wait_recv()
        if m > 0:
            e_buf[d, s, m - 1] = encode(decode(r_buf[d, s, m]) + p_buf[s, rs_owner(d, m)])
            rs_copy(d, s, m).start()

    def x_copy(i):
        return remote(fx_buf.at[i], x_buf.at[i], x_s.at[i], x_r.at[i], x_to)

    def t_copy(i):
        return remote(t_buf.at[i], s_buf.at[i], t_s.at[i], t_r.at[i], sibling)

    weights = set()

    def matmul(s):
        i = s // 2
        if i not in weights:
            weights.add(i)
            w_local(i).wait()
            w_send(i).wait_recv()
        block = jnp.concatenate([a_buf[s, k] for k in range(NZ)], axis=1)
        for side in range(2):
            part = jnp.dot(block, w_buf[side, i], preferred_element_type=F32)
            p_buf[s, :, side * rows:(side + 1) * rows] = part.reshape(NY, rows, ab)

    def final(s):
        i = s // 2
        total = p_buf[s, y] + decode(r_buf[0, s, 0]) + decode(r_buf[1, s, 0])
        if s % 2 == 0:
            fx_buf[i] = total
            x_copy(i).start()
        else:
            x_copy(i).wait_recv()
            done = (total + x_buf[i]).astype(jnp.bfloat16)
            out[first + i] = done[:rows]
            t_buf[i] = done[rows:]
            t_copy(i).start()

    def gather_step(d, s, k):
        ag_wait(d, s, k)
        if k < ag_hops(d, s):
            ag_start(d, s, k + 1)
        if s < 2 * NF:
            xg_copy(d, s, k, x_hi).start()

    def swapped(i):
        for d in range(2):
            for k in range(1, ag_hops(d, 2 * i) + 1):
                xg_copy(d, 2 * i, k, 1 - x_hi).wait_recv()

    def gather_first(s):
        for d in range(2):
            ag_start(d, s, 1)

    def multiply(s):
        matmul(s)
        for d in range(2):
            rs_start(d, s)

    def sum_step(d, s, k):
        rs_arrive(d, s, rs_hops(d, s) - k)

    steps = (prep, gather_first, gather_step, multiply, sum_step, final, swapped)
    for kind, *which in ORDER:
        steps[kind](*which)

    for i in range(nh):
        t_copy(i).wait_recv()
        out[other + i] = s_buf[i]

    for i in range(nh):
        for d in range(3):
            lam_send(d, i).wait_send()
        w_send(i).wait_send()
        x_copy(i).wait_send()
        t_copy(i).wait_send()
    for s in range(nst):
        for d in range(2):
            for k in range(1, ag_hops(d, s) + 1 if s >= 2 * NF or s % 2 == 0 else 1):
                ag_copy(d, s, k, k - 1).wait_send()
                if s < 2 * NF:
                    xg_copy(d, s, k, x_hi).wait_send()
            for m in range(1, rs_hops(d, s) + 1):
                rs_copy(d, s, m).wait_send()


def per_device(lam, integrals, block_mask):
    nirrep, ij, cb = lam.shape
    _, cd, ab = integrals.shape
    nh = nirrep // 2
    nst = 2 * nh
    half = ij // 2
    rows = half // NY
    bf = jnp.bfloat16
    dma = pltpu.SemaphoreType.DMA
    any_spec = pl.BlockSpec(memory_space=pl.ANY)
    return pl.pallas_call(
        functools.partial(kernel, nh),
        out_shape=jax.ShapeDtypeStruct((nirrep, rows, ab), bf),
        in_specs=[any_spec, any_spec, pl.BlockSpec(memory_space=pltpu.SMEM)],
        out_specs=pl.BlockSpec(memory_space=pltpu.VMEM),
        scratch_shapes=[
            pltpu.VMEM((nh, NQ, cb, ij), bf),
            pltpu.VMEM((nst, NZ, half, NQ * cb), bf),
            pltpu.VMEM((2, nh, cd, ab), bf),
            pltpu.VMEM((nst, NY, 2 * rows, ab), F32),
            pltpu.VMEM((2, nst, 4, 2 * rows + SCALE_ROWS, ab), I16),
            pltpu.VMEM((2, nst, 4, 2 * rows + SCALE_ROWS, ab), I16),
            pltpu.VMEM((nh, 2 * rows, ab), F32),
            pltpu.VMEM((nh, 2 * rows, ab), F32),
            pltpu.VMEM((nh, rows, ab), bf),
            pltpu.VMEM((nh, rows, ab), bf),
            dma((3, nh)), dma((3, nh)), dma((nh,)),
            dma((nh,)), dma((nh,)), dma((nh,)),
            dma((2, nst, 4)), dma((2, nst, 4)),
            dma((2, NF, 4)), dma((2, NF, 4)),
            dma((2, nst, 4)), dma((2, nst, 4)),
            dma((nh,)), dma((nh,)),
            dma((nh,)), dma((nh,)),
        ],
        compiler_params=pltpu.CompilerParams(collective_id=0, has_side_effects=True),
    )(lam.transpose(0, 2, 1), integrals, block_mask)


def solution(mesh):
    return jax.shard_map(
        per_device,
        mesh=mesh,
        in_specs=(P(None, None, ("rep", "loop")), P(None, "rep", "loop"), P(None, "rep")),
        out_specs=P(None, "rep", "loop"),
        check_vma=False,
    )
```

```python
import functools

import jax
import jax.numpy as jnp
from jax import lax
from jax.experimental import pallas as pl
from jax.experimental.pallas import tpu as pltpu
from jax.sharding import PartitionSpec as P

MESH = pl.DeviceIdType.MESH
NZ = 8
NY = 8
NF = 2
NQ = 4
F32 = jnp.float32
I16 = jnp.int16
SCALE_ROWS = 8

ORDER = (
    (0, 0), (1, 0), (0, 1), (1, 2), (0, 2), (1, 4), (2, 1, 0, 1), (2, 0, 0, 1), (1, 5), (2, 1, 2, 1), (0, 3),
    (1, 6), (2, 0, 2, 1), (2, 1, 0, 2), (2, 0, 0, 2), (1, 7), (2, 0, 6, 1), (2, 1, 2, 2), (2, 0, 2, 2),
    (2, 1, 0, 3), (2, 1, 4, 1), (2, 0, 0, 3), (2, 0, 4, 1), (2, 1, 6, 1), (2, 1, 2, 3), (2, 1, 7, 1),
    (2, 0, 6, 2), (2, 1, 4, 2), (2, 0, 7, 1), (2, 0, 0, 4), (2, 0, 2, 3), (2, 1, 5, 1), (2, 0, 4, 2),
    (2, 1, 2, 4), (2, 1, 7, 2), (2, 0, 5, 1), (6, 0), (2, 0, 6, 3), (2, 1, 6, 2), (3, 0), (3, 1),
    (2, 0, 4, 3), (2, 1, 5, 2), (6, 1), (2, 0, 7, 2), (3, 3), (3, 2), (4, 0, 0, 1), (2, 1, 6, 3),
    (2, 0, 6, 4), (2, 1, 7, 3), (2, 0, 5, 2), (4, 1, 0, 1), (2, 1, 4, 3), (3, 6), (4, 0, 1, 1), (2, 1, 5, 3),
    (4, 1, 1, 1), (2, 0, 4, 4), (3, 4), (4, 0, 2, 1), (4, 1, 3, 1), (4, 1, 0, 2), (2, 0, 7, 3), (4, 0, 0, 2),
    (2, 0, 5, 3), (2, 1, 7, 4), (4, 1, 2, 1), (4, 0, 6, 1), (3, 7), (4, 0, 4, 1), (2, 1, 5, 4), (4, 1, 6, 1),
    (3, 5), (4, 0, 2, 2), (4, 1, 4, 1), (4, 0, 3, 1), (4, 1, 3, 2), (4, 0, 6, 2), (4, 0, 0, 3), (4, 1, 0, 3),
    (4, 1, 7, 1), (4, 1, 2, 2), (4, 0, 4, 2), (4, 1, 5, 1), (4, 0, 2, 3), (4, 1, 1, 2), (4, 0, 7, 1),
    (4, 1, 6, 2), (4, 0, 6, 3), (4, 1, 7, 2), (4, 0, 5, 1), (4, 0, 0, 4), (5, 0), (4, 1, 4, 2), (4, 1, 2, 3),
    (4, 0, 4, 3), (4, 1, 5, 2), (4, 0, 1, 2), (4, 0, 2, 4), (5, 2), (4, 0, 3, 2), (4, 1, 1, 3), (4, 1, 3, 3),
    (4, 0, 6, 4), (4, 1, 6, 3), (5, 6), (4, 0, 7, 2), (4, 1, 7, 3), (4, 0, 5, 2), (4, 1, 4, 3), (4, 0, 4, 4),
    (5, 4), (4, 1, 5, 3), (4, 0, 3, 3), (4, 1, 7, 4), (4, 1, 3, 4), (4, 0, 1, 3), (5, 3), (4, 1, 1, 4),
    (4, 0, 7, 3), (5, 1), (4, 0, 5, 3), (5, 7), (4, 1, 5, 4), (5, 5),
)


def encode(v):
    top = jnp.maximum(jnp.max(jnp.abs(v), axis=0, keepdims=True), 1e-37)
    c = jnp.maximum(jnp.ceil(jnp.log2(top)) - 15, -126)
    q = jnp.clip(jnp.round(v * jnp.exp2(-c)), -32767, 32767)
    coded = jnp.concatenate([q, jnp.broadcast_to(c, (SCALE_ROWS, v.shape[1]))], axis=0)
    return coded.astype(jnp.int32).astype(I16)


def decode(coded):
    f = coded.astype(jnp.int32).astype(F32)
    rows = f.shape[0] - SCALE_ROWS
    return f[:rows] * jnp.exp2(f[rows:rows + 1])


def kernel(nh, lam, w, mask, out, q_buf, a_buf, w_buf, p_buf, e_buf, r_buf, x_buf, fx_buf, t_buf, s_buf,
           lam_s, lam_r, lam_l, w_s, w_r, w_l, ag_s, ag_r, xg_s, xg_r, rs_s, rs_r, x_s, x_r, t_s, t_r):
    nst = 2 * nh
    ij = lam.shape[2]
    half = ij // 2
    ab = w.shape[2]
    rows = half // NY

    loop = lax.axis_index("loop")
    rep = lax.axis_index("rep")
    z = loop // NQ
    quad = loop % NQ
    core = loop % 2
    x_hi = quad // 2
    x_lo = rep // NY
    y = rep % NY
    first = core * nh
    other = (1 - core) * nh

    def dev(loop_to, rep_to):
        return {"loop": loop_to, "rep": rep_to}

    sibling = dev(z * NQ + x_hi * 2 + (1 - core), rep)
    quads = (
        (sibling, other),
        (dev(z * NQ + (1 - x_hi) * 2 + core, rep), first),
        (dev(z * NQ + (1 - x_hi) * 2 + (1 - core), rep), other),
    )
    z_to = (dev((z + 1) % NZ * NQ + quad, rep), dev((z + NZ - 1) % NZ * NQ + quad, rep))
    y_to = (dev(loop, x_lo * NY + (y + 1) % NY), dev(loop, x_lo * NY + (y + NY - 1) % NY))
    x_to = dev(loop, (1 - x_lo) * NY + y)

    def remote(src, dst, send, recv, to):
        return pltpu.make_async_remote_copy(
            src_ref=src, dst_ref=dst, send_sem=send, recv_sem=recv, device_id=to, device_id_type=MESH)

    def lam_local(i):
        return pltpu.make_async_copy(lam.at[first + i], q_buf.at[i, quad], lam_l.at[i])

    def w_local(i):
        return pltpu.make_async_copy(w.at[first + i], w_buf.at[0, i], w_l.at[i])

    for i in range(nh):
        lam_local(i).start()
    for i in range(nh):
        w_local(i).start()

    barrier = pltpu.get_barrier_semaphore()
    peers = [to for to, _ in quads] + list(z_to) + list(y_to) + [x_to]
    for to in peers:
        pl.semaphore_signal(barrier, inc=1, device_id=to, device_id_type=MESH)
    pl.semaphore_wait(barrier, len(peers))

    def lam_send(d, i):
        to, h0 = quads[d]
        return remote(lam.at[h0 + i], q_buf.at[i, quad], lam_s.at[d, i], lam_r.at[d, i], to)

    def w_send(i):
        return remote(w.at[other + i], w_buf.at[1, i], w_s.at[i], w_r.at[i], sibling)

    for i in range(nh):
        for d in (1, 2, 0):
            lam_send(d, i).start()
    for i in range(nh):
        w_send(i).start()

    def prep(i):
        lam_local(i).wait()
        for d in range(3):
            lam_send(d, i).wait_recv()
        parts = []
        for k in range(NQ):
            live = mask[first + i, z * NQ + k].astype(F32)
            parts.append(q_buf[i, k].astype(F32) * live)
        block = jnp.concatenate(parts, axis=0).T.astype(jnp.bfloat16)
        a_buf[2 * i + (1 - x_lo), z] = block[:half]
        a_buf[2 * i + x_lo, z] = block[half:]

    def ag_hops(d, s):
        return NZ // 2 if d == (s // 2 if s < 2 * NF else s) % 2 else NZ // 2 - 1

    def ag_from(d, back):
        return (z + NZ - back) % NZ if d == 0 else (z + back) % NZ

    def ag_copy(d, s, k, back):
        block = a_buf.at[s + x_hi if s < 2 * NF else s, ag_from(d, back)]
        return remote(block, block, ag_s.at[d, s, k - 1], ag_r.at[d, s, k - 1], z_to[d])

    def ag_start(d, s, k):
        ag_copy(d, s, k, k - 1).start()

    def ag_wait(d, s, k):
        ag_copy(d, s, k, k).wait_recv()

    def xg_copy(d, s, k, side):
        block = a_buf.at[s + side, ag_from(d, k)]
        return remote(block, block, xg_s.at[d, s // 2, k - 1], xg_r.at[d, s // 2, k - 1], quads[1][0])

    def rs_hops(d, s):
        return NY // 2 if d == s % 2 else NY // 2 - 1

    def rs_owner(d, m):
        return (y + m) % NY if d == 0 else (y + NY - m) % NY

    def rs_copy(d, s, m):
        return remote(e_buf.at[d, s, m - 1], r_buf.at[d, s, m - 1], rs_s.at[d, s, m - 1], rs_r.at[d, s, m - 1], y_to[d])

    def rs_start(d, s):
        m = rs_hops(d, s)
        e_buf[d, s, m - 1] = encode(p_buf[s, rs_owner(d, m)])
        rs_copy(d, s, m).start()

    def rs_arrive(d, s, m):
        rs_copy(d, s, m + 1).wait_recv()
        if m > 0:
            e_buf[d, s, m - 1] = encode(decode(r_buf[d, s, m]) + p_buf[s, rs_owner(d, m)])
            rs_copy(d, s, m).start()

    def x_copy(i):
        return remote(fx_buf.at[i], x_buf.at[i], x_s.at[i], x_r.at[i], x_to)

    def t_copy(i):
        return remote(t_buf.at[i], s_buf.at[i], t_s.at[i], t_r.at[i], sibling)

    weights = set()

    def matmul(s):
        i = s // 2
        if i not in weights:
            weights.add(i)
            w_local(i).wait()
            w_send(i).wait_recv()
        block = jnp.concatenate([a_buf[s, k] for k in range(NZ)], axis=1)
        for side in range(2):
            part = jnp.dot(block, w_buf[side, i], preferred_element_type=F32)
            p_buf[s, :, side * rows:(side + 1) * rows] = part.reshape(NY, rows, ab)

    def final(s):
        i = s // 2
        total = p_buf[s, y] + decode(r_buf[0, s, 0]) + decode(r_buf[1, s, 0])
        if s % 2 == 0:
            fx_buf[i] = total
            x_copy(i).start()
        else:
            x_copy(i).wait_recv()
            done = (total + x_buf[i]).astype(jnp.bfloat16)
            out[first + i] = done[:rows]
            t_buf[i] = done[rows:]
            t_copy(i).start()

    def gather_step(d, s, k):
        ag_wait(d, s, k)
        if k < ag_hops(d, s):
            ag_start(d, s, k + 1)
        if s < 2 * NF:
            xg_copy(d, s, k, x_hi).start()

    def swapped(i):
        for d in range(2):
            for k in range(1, ag_hops(d, 2 * i) + 1):
                xg_copy(d, 2 * i, k, 1 - x_hi).wait_recv()

    def gather_first(s):
        for d in range(2):
            ag_start(d, s, 1)

    def multiply(s):
        matmul(s)
        for d in range(2):
            rs_start(d, s)

    def sum_step(d, s, k):
        rs_arrive(d, s, rs_hops(d, s) - k)

    steps = (prep, gather_first, gather_step, multiply, sum_step, final, swapped)
    for kind, *which in ORDER:
        steps[kind](*which)

    for i in range(nh):
        t_copy(i).wait_recv()
        out[other + i] = s_buf[i]

    for i in range(nh):
        for d in range(3):
            lam_send(d, i).wait_send()
        w_send(i).wait_send()
        x_copy(i).wait_send()
        t_copy(i).wait_send()
    for s in range(nst):
        for d in range(2):
            for k in range(1, ag_hops(d, s) + 1 if s >= 2 * NF or s % 2 == 0 else 1):
                ag_copy(d, s, k, k - 1).wait_send()
                if s < 2 * NF:
                    xg_copy(d, s, k, x_hi).wait_send()
            for m in range(1, rs_hops(d, s) + 1):
                rs_copy(d, s, m).wait_send()


def per_device(lam, integrals, block_mask):
    nirrep, ij, cb = lam.shape
    _, cd, ab = integrals.shape
    nh = nirrep // 2
    nst = 2 * nh
    half = ij // 2
    rows = half // NY
    bf = jnp.bfloat16
    dma = pltpu.SemaphoreType.DMA
    any_spec = pl.BlockSpec(memory_space=pl.ANY)
    return pl.pallas_call(
        functools.partial(kernel, nh),
        out_shape=jax.ShapeDtypeStruct((nirrep, rows, ab), bf),
        in_specs=[any_spec, any_spec, pl.BlockSpec(memory_space=pltpu.SMEM)],
        out_specs=pl.BlockSpec(memory_space=pltpu.VMEM),
        scratch_shapes=[
            pltpu.VMEM((nh, NQ, cb, ij), bf),
            pltpu.VMEM((nst, NZ, half, NQ * cb), bf),
            pltpu.VMEM((2, nh, cd, ab), bf),
            pltpu.VMEM((nst, NY, 2 * rows, ab), F32),
            pltpu.VMEM((2, nst, 4, 2 * rows + SCALE_ROWS, ab), I16),
            pltpu.VMEM((2, nst, 4, 2 * rows + SCALE_ROWS, ab), I16),
            pltpu.VMEM((nh, 2 * rows, ab), F32),
            pltpu.VMEM((nh, 2 * rows, ab), F32),
            pltpu.VMEM((nh, rows, ab), bf),
            pltpu.VMEM((nh, rows, ab), bf),
            dma((3, nh)), dma((3, nh)), dma((nh,)),
            dma((nh,)), dma((nh,)), dma((nh,)),
            dma((2, nst, 4)), dma((2, nst, 4)),
            dma((2, NF, 4)), dma((2, NF, 4)),
            dma((2, nst, 4)), dma((2, nst, 4)),
            dma((nh,)), dma((nh,)),
            dma((nh,)), dma((nh,)),
        ],
        compiler_params=pltpu.CompilerParams(collective_id=0, has_side_effects=True),
    )(lam.transpose(0, 2, 1), integrals, block_mask)


def solution(mesh):
    return jax.shard_map(
        per_device,
        mesh=mesh,
        in_specs=(P(None, None, ("rep", "loop")), P(None, "rep", "loop"), P(None, "rep")),
        out_specs=P(None, "rep", "loop"),
        check_vma=False,
    )
```
